32 devices in a mesh: gx: 4 (over x, core), gy: 2 (over y), gz: 4 (over z).
Axes of the slice: x: 2, y: 2, z: 4, core: 2. Of those that a mesh axis runs over, the one named last changes fastest.
Arguments:
- local_schur: float32 [1024, 1024], replicated, may hold values from -1 to 4, as said below
- block_inverse: float32 [1024, 1024], replicated, may hold values from -1 to 1, as said below
- coefficient: float32 [4, 2, 4], P('gx', 'gy', 'gz'), may hold values from 0.3 to 3
- face_index: int32 [1024], replicated, may hold values from 0 to 1023, each once
- right_side: float32 [4, 2, 4, 1024, 128], P('gx', 'gy', 'gz'), may hold values from -6 to 6
Outputs:
- solution: float32 [4, 2, 4, 1024, 128], P('gx', 'gy', 'gz')
- residual: float32 [4, 2, 4, 1024, 128], P('gx', 'gy', 'gz')
The draws below stay inside these ranges and needn't reach their ends.
Inputs may be any that keep to these rules, and one draw needn't show every extreme that they name: `local_schur`: symmetric positive definite. `block_inverse`: symmetric positive definite. `face_index`: entries k * 128 to (k + 1) * 128 - 1 list face k's unknowns as in the reference program; the last 256 entries are unknowns of one subdomain alone.
All inputs are finite; a program needn't handle non-finite values.
Results may differ from the reference program's by a relative error of at most 0.00022.
Values sent between devices are 32-bit elements; how exact they have to be, the bound alone decides.
A program may use at most 64 MiB of HBM per device.

```python
import math
import jax
import jax.numpy as jnp
from jax import lax

W = 1024
FACE = 128
R = 128
PX = 4
PY = 2
PZ = 4


def symmetric_block(key, spread, low, high):
    first, second = jax.random.split(key)
    noise = jax.random.normal(first, (W, W), jnp.float32) * (spread / math.sqrt(W))
    diagonal = jax.random.uniform(second, (W,), jnp.float32, low, high)
    return noise + noise.T + jnp.diag(diagonal)


def draw_local_schur(key, part):
    return symmetric_block(jax.random.fold_in(key, 11), 0.32, 1.5, 3.0)


def draw_block_inverse(key, part):
    return symmetric_block(jax.random.fold_in(key, 23), 0.07, 0.3, 0.7)


def block_scale(rng, shape, cuts, low, top_value):
    def one(dim, parts):
        heights = jax.random.uniform(jax.random.fold_in(jax.random.fold_in(rng, 6), dim), (parts,), jnp.float32, low / len(cuts), top_value / len(cuts))
        return jnp.repeat(jnp.exp(heights), shape[dim] // parts).reshape((-1,) + (1,) * (len(shape) - dim - 1))

    level = one(*cuts[0])
    for cut in cuts[1:]:
        level = level * one(*cut)
    return level


def scatter_about(own_key, shape, scale, most, pieces=(), kind=jnp.bfloat16):
    values = jax.random.normal(own_key, shape, jnp.float32) * scale
    if len(pieces) > 0:
        values = block_scale(own_key, shape, pieces, -0.22, 0.18) * values
    return jnp.clip(values, min=-most, max=most).astype(kind)


def setup_inputs(seed: int = 0) -> dict:
    key_of = jax.random.split(jax.random.key(seed), 6)
    local_schur = draw_local_schur(jax.random.fold_in(key_of[5], 71), 0)
    block_inverse = draw_block_inverse(jax.random.fold_in(key_of[5], 71), 0)
    coefficient = jnp.clip(jnp.exp(math.log(3.0) - 2.3025851 * jax.random.uniform(key_of[2], (PX, PY, PZ), jnp.float32) ** block_scale(key_of[2], (PX, PY, PZ), ((0, 4), (1, 2), (2, 4)), -0.2, 0.2)), 0.3, 3.0)
    face_index = jax.random.permutation(key_of[3], W).astype(jnp.int32)
    right_side = scatter_about(key_of[4], (PX, PY, PZ, W, R), 1.0, 6.0, ((0, 4), (1, 2), (2, 4)), jnp.float32)
    return {"local_schur": local_schur, "block_inverse": block_inverse, "coefficient": coefficient, "face_index": face_index, "right_side": right_side}


def shift_down(arr, axis):
    pad = [(0, 0)] * arr.ndim
    pad[axis] = (1, 0)
    padded = jnp.pad(arr, pad)
    return lax.slice_in_dim(padded, 0, arr.shape[axis], axis=axis)


def shift_up(arr, axis):
    pad = [(0, 0)] * arr.ndim
    pad[axis] = (0, 1)
    padded = jnp.pad(arr, pad)
    return lax.slice_in_dim(padded, 1, arr.shape[axis] + 1, axis=axis)


def assemble(vec, flat_index):
    faces = vec[:, :, :, flat_index, :].reshape(PX, PY, PZ, 6, FACE, vec.shape[-1])
    adds = []
    for axis in range(3):
        minus = faces[:, :, :, 2 * axis]
        plus = faces[:, :, :, 2 * axis + 1]
        adds.append(shift_down(plus, axis))
        adds.append(shift_up(minus, axis))
    stacked = jnp.stack(adds, axis=3).reshape(PX, PY, PZ, 6 * FACE, vec.shape[-1])
    return vec.at[:, :, :, flat_index, :].add(stacked)


def make_weight(face_rows):
    weight = jnp.ones((PX, PY, PZ, W), jnp.float32)
    counts = (PX, PY, PZ)
    for axis in range(3):
        position = lax.broadcasted_iota(jnp.int32, (PX, PY, PZ, 1), axis)
        lower = jnp.where(position > 0, 0.5, 1.0).astype(jnp.float32)
        upper = jnp.where(position < counts[axis] - 1, 0.5, 1.0).astype(jnp.float32)
        weight = weight.at[:, :, :, face_rows[2 * axis]].set(jnp.broadcast_to(lower, (PX, PY, PZ, FACE)))
        weight = weight.at[:, :, :, face_rows[2 * axis + 1]].set(jnp.broadcast_to(upper, (PX, PY, PZ, FACE)))
    return weight


def reference(local_schur, block_inverse, coefficient, face_index, right_side):
    face_rows = face_index[:6 * FACE].reshape(6, FACE)
    flat_index = face_rows.reshape(-1)
    weight = make_weight(face_rows)[..., None]
    scale = coefficient[..., None, None]

    def product(matrix, vec):
        return jnp.einsum('ij,abcjr->abcir', matrix, vec, precision=lax.Precision.HIGHEST)

    def apply_operator(vec):
        return assemble(product(local_schur, vec) * scale, flat_index)

    def apply_precond(vec):
        return assemble(product(block_inverse, vec) / scale, flat_index)

    def dot(left, right):
        return jnp.sum(weight * left * right, axis=(0, 1, 2, 3))

    rhs = assemble(right_side, flat_index)
    solution = jnp.zeros_like(rhs)
    residual = rhs
    precond = apply_precond(residual)
    norm_now = dot(residual, precond)
    direction = precond
    for step in range(2):
        image = apply_operator(direction)
        alpha = norm_now / dot(direction, image)
        solution = solution + alpha * direction
        residual = residual - alpha * image
        if step == 0:
            precond = apply_precond(residual)
            norm_next = dot(residual, precond)
            direction = precond + (norm_next / norm_now) * direction
            norm_now = norm_next
    return solution, residual
```

```python
import functools
import jax
import jax.numpy as jnp
from jax import lax
from jax.experimental import pallas as pl
from jax.experimental.pallas import tpu as pltpu
from jax.sharding import PartitionSpec as P

AXES = ("gx", "gy", "gz")
MESH = pl.DeviceIdType.MESH
F32 = jnp.float32
BF16 = jnp.bfloat16


def split(x):
    hi = x.astype(BF16)
    return hi, (x - hi.astype(F32)).astype(BF16)


def halves(x):
    hi, lo = split(x)
    return jnp.concatenate([hi, lo], axis=1)


def dot(a, b):
    return jnp.dot(a, b, preferred_element_type=F32)


def kernel(
    sizes, stages, scale_ref, index_ref, side_hbm, inv_hbm, schur_hbm, sol_ref, res_ref,
    raw, side, mats, gather, scatter, send, recv, vecs, dsend, drecv,
    copy_sem, ssem, rsem, dssem, drsem,
):
    width, cols = side.shape
    face = width // 8
    position = [lax.axis_index(name) for name in AXES]

    load_side = pltpu.make_async_copy(side_hbm, side, copy_sem.at[0])
    load_inv = pltpu.make_async_copy(inv_hbm, raw.at[0], copy_sem.at[1])
    load_schur = pltpu.make_async_copy(schur_hbm, raw.at[1], copy_sem.at[2])
    load_side.start()
    load_inv.start()
    load_schur.start()

    def peer(stage, offset):
        count = 1
        me = 0
        for axis in stage:
            count *= sizes[axis]
            me = me * sizes[axis] + position[axis]
        other = lax.rem(me + offset, count)
        device = {}
        for axis in reversed(stage):
            device[AXES[axis]] = lax.rem(other, sizes[axis])
            other = lax.div(other, sizes[axis])
        return device

    counts = []
    for stage in stages:
        count = 1
        for axis in stage:
            count *= sizes[axis]
        counts.append(count)
    bases = [sum(counts[:i]) for i in range(len(counts))]

    barrier = pltpu.get_barrier_semaphore()
    for stage, count in zip(stages, counts):
        @pl.loop(1, count)
        def _(offset, stage=stage):
            pl.semaphore_signal(
                barrier, inc=1, device_id=peer(stage, offset), device_id_type=MESH
            )

    for k in range(6):
        row = index_ref[k : k + 1, :]
        down = lax.broadcasted_iota(jnp.int32, (width, face), 0)
        scatter[:, k * face : (k + 1) * face] = jnp.where(down == row, 1.0, 0.0).astype(BF16)
        column = jnp.broadcast_to(row.astype(F32), (face, face)).T
        for m in range(width // face):
            across = (lax.broadcasted_iota(jnp.int32, (face, face), 1) + m * face).astype(F32)
            gather[k * face : (k + 1) * face, m * face : (m + 1) * face] = jnp.where(
                across == column, 1.0, 0.0
            ).astype(BF16)

    for axis in range(3):
        @pl.when(position[axis] == 0)
        def _(axis=axis):
            for step in range(5):
                recv[step, 2 * axis] = jnp.zeros((face, cols), F32)

        @pl.when(position[axis] == sizes[axis] - 1)
        def _(axis=axis):
            for step in range(5):
                recv[step, 2 * axis + 1] = jnp.zeros((face, cols), F32)

    def face_copy(step, axis, up):
        mine, theirs = (2 * axis + 1, 2 * axis) if up else (2 * axis, 2 * axis + 1)
        return pltpu.make_async_remote_copy(
            src_ref=send.at[step, mine],
            dst_ref=recv.at[step, theirs],
            send_sem=ssem.at[step, mine],
            recv_sem=rsem.at[step, theirs],
            device_id={AXES[axis]: position[axis] + (1 if up else -1)},
            device_id_type=MESH,
        )

    def post(step, vec):
        out = dot(gather[...], halves(vec))
        out = out[:, :cols] + out[:, cols:]
        for k in range(6):
            send[step, k] = out[k * face : (k + 1) * face]

    def start(step):
        for axis in range(3):
            @pl.when(position[axis] < sizes[axis] - 1)
            def _(axis=axis):
                face_copy(step, axis, True).start()

            @pl.when(position[axis] > 0)
            def _(axis=axis):
                face_copy(step, axis, False).start()

    def arrived(step):
        for axis in range(3):
            @pl.when(position[axis] > 0)
            def _(axis=axis):
                face_copy(step, axis, True).wait_recv()

            @pl.when(position[axis] < sizes[axis] - 1)
            def _(axis=axis):
                face_copy(step, axis, False).wait_recv()

        got = recv[step].reshape(6 * face, cols)
        out = dot(scatter[...], halves(got))
        return out[:, :cols] + out[:, cols:]

    def load_matrix(which):
        hi, lo = split(raw[which])
        mats[which, :width] = hi
        mats[which, width:] = lo

    def product(which, vec):
        out = dot(mats[which], halves(vec))
        return out[:width, :cols] + (out[:width, cols:] + out[width:, :cols])

    def local_dot(left, right):
        return jnp.sum(left * right, axis=0, keepdims=True)

    def sum_copy(turn, level, offset):
        slot = bases[level] + offset
        return pltpu.make_async_remote_copy(
            src_ref=dsend.at[turn, level],
            dst_ref=drecv.at[turn, slot],
            send_sem=dssem.at[turn, slot],
            recv_sem=drsem.at[turn, slot],
            device_id=peer(stages[level], offset),
            device_id_type=MESH,
        )

    def sum_start(turn, level):
        @pl.loop(1, counts[level])
        def _(offset):
            sum_copy(turn, level, offset).start()

    def sum_begin(turn, first, second):
        dsend[turn, 0] = jnp.concatenate([first, second, jnp.zeros((6, cols), F32)], axis=0)
        sum_start(turn, 0)

    def sum_end(turn):
        for level, count in enumerate(counts):
            @pl.loop(1, count)
            def _(offset, level=level):
                sum_copy(turn, level, offset).wait_recv()

            total = dsend[turn, level] + jnp.sum(
                drecv[turn, bases[level] + 1 : bases[level] + count], axis=0
            )
            if level + 1 < len(counts):
                dsend[turn, level + 1] = total
                sum_start(turn, level + 1)
        return total[0:1], total[1:2]

    scale = jnp.full((1, cols), scale_ref[0, 0], F32)
    inverse = 1.0 / scale
    rhs, pre_part, pre, img_part, img, pre2_part, pre2, img2_part = [vecs.at[i] for i in range(8)]

    load_side.wait()
    post(0, side[...])
    pl.semaphore_wait(barrier, sum(counts) - len(counts))
    start(0)
    load_inv.wait()
    load_matrix(0)
    rhs[...] = side[...] + arrived(0)
    pre_part[...] = product(0, rhs[...]) * inverse
    post(1, pre_part[...])
    start(1)
    first = local_dot(rhs[...], pre_part[...])
    load_schur.wait()
    load_matrix(1)
    pre[...] = pre_part[...] + arrived(1)
    img_part[...] = product(1, pre[...]) * scale
    post(2, img_part[...])
    start(2)
    second = local_dot(pre[...], img_part[...])
    sum_begin(0, first, second)
    img[...] = img_part[...] + arrived(2)
    pre2_part[...] = product(0, img[...]) * inverse
    post(3, pre2_part[...])
    start(3)
    pre2[...] = pre2_part[...] + arrived(3)
    img2_part[...] = product(1, pre2[...]) * scale
    norm_now, along = sum_end(0)
    alpha = norm_now / along
    res_ref[...] = rhs[...] - alpha * img[...]
    sol_ref[...] = pre[...] - alpha * pre2[...]
    sum_begin(
        1,
        local_dot(res_ref[...], pre_part[...] - alpha * pre2_part[...]),
        local_dot(sol_ref[...], img_part[...] - alpha * img2_part[...]),
    )
    post(4, img2_part[...])
    start(4)
    image2 = img[...] - alpha * (img2_part[...] + arrived(4))
    norm_next, along = sum_end(1)
    ratio = norm_next / norm_now
    alpha2 = norm_next / (along - ratio * norm_next / alpha)
    sol_ref[...] = alpha * pre[...] + alpha2 * (sol_ref[...] + ratio * pre[...])
    res_ref[...] = res_ref[...] - alpha2 * (image2 + ratio * img[...])

    for step in range(5):
        for axis in range(3):
            @pl.when(position[axis] < sizes[axis] - 1)
            def _(axis=axis):
                face_copy(step, axis, True).wait_send()

            @pl.when(position[axis] > 0)
            def _(axis=axis):
                face_copy(step, axis, False).wait_send()
    for turn in range(2):
        for level, count in enumerate(counts):
            @pl.loop(1, count)
            def _(offset, level=level):
                sum_copy(turn, level, offset).wait_send()


def on_device(local_schur, block_inverse, coefficient, face_index, right_side):
    width = local_schur.shape[0]
    face = width // 8
    cols = right_side.shape[-1]
    sizes = [lax.axis_size(name) for name in AXES]
    total = sizes[0] * sizes[1] * sizes[2]
    stages = [(0, 1, 2)] if total <= 64 else [(0,), (1,), (2,)]
    slots = total if total <= 64 else sum(sizes)
    out = jax.ShapeDtypeStruct((width, cols), F32)
    sol, res = pl.pallas_call(
        functools.partial(kernel, sizes, stages),
        out_shape=(out, out),
        in_specs=[
            pl.BlockSpec(memory_space=pltpu.SMEM),
            pl.BlockSpec(memory_space=pltpu.VMEM),
            pl.BlockSpec(memory_space=pl.ANY),
            pl.BlockSpec(memory_space=pl.ANY),
            pl.BlockSpec(memory_space=pl.ANY),
        ],
        out_specs=(pl.BlockSpec(memory_space=pltpu.VMEM), pl.BlockSpec(memory_space=pltpu.VMEM)),
        scratch_shapes=[
            pltpu.VMEM((2, width, width), F32),
            pltpu.VMEM((width, cols), F32),
            pltpu.VMEM((2, 2 * width, width), BF16),
            pltpu.VMEM((6 * face, width), BF16),
            pltpu.VMEM((width, 6 * face), BF16),
            pltpu.VMEM((5, 6, face, cols), F32),
            pltpu.VMEM((5, 6, face, cols), F32),
            pltpu.VMEM((8, width, cols), F32),
            pltpu.VMEM((2, len(stages), 8, cols), F32),
            pltpu.VMEM((2, slots, 8, cols), F32),
            pltpu.SemaphoreType.DMA((3,)),
            pltpu.SemaphoreType.DMA((5, 6)),
            pltpu.SemaphoreType.DMA((5, 6)),
            pltpu.SemaphoreType.DMA((2, slots)),
            pltpu.SemaphoreType.DMA((2, slots)),
        ],
        compiler_params=pltpu.CompilerParams(
            collective_id=0, has_side_effects=True, vmem_limit_bytes=60 * 1024 * 1024
        ),
        name="schur_pcg",
    )(
        coefficient.reshape(1, 1),
        face_index.reshape(8, face),
        right_side.reshape(width, cols),
        block_inverse,
        local_schur,
    )
    return sol.reshape(1, 1, 1, width, cols), res.reshape(1, 1, 1, width, cols)


def solution(mesh):
    placed = (P(), P(), P(*AXES), P(), P(*AXES, None, None))
    return jax.shard_map(
        on_device,
        mesh=mesh,
        in_specs=placed,
        out_specs=(P(*AXES, None, None), P(*AXES, None, None)),
        check_vma=False,
    )
```

```python
import functools
import jax
import jax.numpy as jnp
from jax import lax
from jax.experimental import pallas as pl
from jax.experimental.pallas import tpu as pltpu
from jax.sharding import PartitionSpec as P

AXES = ("gx", "gy", "gz")
MESH = pl.DeviceIdType.MESH
F32 = jnp.float32
BF16 = jnp.bfloat16


def split(x):
    hi = x.astype(BF16)
    return hi, (x - hi.astype(F32)).astype(BF16)


def halves(x):
    hi, lo = split(x)
    return jnp.concatenate([hi, lo], axis=1)


def dot(a, b):
    return jnp.dot(a, b, preferred_element_type=F32)


def kernel(
    sizes, stages, scale_ref, order_ref, index_ref, side_hbm, inv_hbm, schur_hbm, sol_ref, res_ref,
    raw_inv, raw_schur, rows, side, mats, gather, scatter, fresh, send, recv, vecs, dsend, drecv,
    copy_sem, ssem, rsem, dssem, drsem,
):
    width, cols = side.shape
    face = width // 8
    position = [lax.axis_index(name) for name in AXES]

    load_side = pltpu.make_async_copy(side_hbm, side, copy_sem.at[0])
    raw = (raw_inv, raw_schur)
    lanes = 128
    tiles = width // lanes

    def matrix_copies(which, source):
        return [
            pltpu.make_async_copy(
                source.at[:, c * lanes : (c + 1) * lanes],
                raw[which].at[:, c, :],
                copy_sem.at[1 + which * tiles + c],
            )
            for c in range(tiles)
        ]

    load_inv = matrix_copies(0, inv_hbm)
    load_schur = matrix_copies(1, schur_hbm)
    load_side.start()
    for copy in load_inv + load_schur:
        copy.start()

    def peer(stage, offset):
        count = 1
        me = 0
        for axis in stage:
            count *= sizes[axis]
            me = me * sizes[axis] + position[axis]
        other = lax.rem(me + offset, count)
        device = {}
        for axis in reversed(stage):
            device[AXES[axis]] = lax.rem(other, sizes[axis])
            other = lax.div(other, sizes[axis])
        return device

    counts = []
    for stage in stages:
        count = 1
        for axis in stage:
            count *= sizes[axis]
        counts.append(count)
    bases = [sum(counts[:i]) for i in range(len(counts))]

    barrier = pltpu.get_barrier_semaphore()
    for stage, count in zip(stages, counts):
        @pl.loop(1, count)
        def _(offset, stage=stage):
            pl.semaphore_signal(
                barrier, inc=1, device_id=peer(stage, offset), device_id_type=MESH
            )

    for k in range(6):
        row = index_ref[k : k + 1, :]
        column = jnp.broadcast_to(row.astype(F32), (face, face)).T
        for m in range(width // face):
            across = (lax.broadcasted_iota(jnp.int32, (face, face), 1) + m * face).astype(F32)
            gather[k * face : (k + 1) * face, m * face : (m + 1) * face] = jnp.where(
                across == column, 1.0, 0.0
            ).astype(BF16)

    for axis in range(3):
        @pl.when(position[axis] == 0)
        def _(axis=axis):
            for step in range(5):
                recv[step, 2 * axis] = jnp.zeros((face, cols), F32)

        @pl.when(position[axis] == sizes[axis] - 1)
        def _(axis=axis):
            for step in range(5):
                recv[step, 2 * axis + 1] = jnp.zeros((face, cols), F32)

    def face_copy(step, axis, up):
        mine, theirs = (2 * axis + 1, 2 * axis) if up else (2 * axis, 2 * axis + 1)
        return pltpu.make_async_remote_copy(
            src_ref=send.at[step, mine],
            dst_ref=recv.at[step, theirs],
            send_sem=ssem.at[step, mine],
            recv_sem=rsem.at[step, theirs],
            device_id={AXES[axis]: position[axis] + (1 if up else -1)},
            device_id_type=MESH,
        )

    def post_side():
        out = dot(gather[...], halves(side[...]))
        out = out[:, :cols] + out[:, cols:]
        for k in range(6):
            send[0, k] = out[k * face : (k + 1) * face]

    def build_scatter():
        for k in range(8):
            row = index_ref[k : k + 1, :]
            down = lax.broadcasted_iota(jnp.int32, (width, face), 0)
            scatter[:, k * face : (k + 1) * face] = jnp.where(down == row, 1.0, 0.0).astype(BF16)

    def start(step, axes):
        for axis in axes:
            @pl.when(position[axis] < sizes[axis] - 1)
            def _(axis=axis):
                face_copy(step, axis, True).start()

            @pl.when(position[axis] > 0)
            def _(axis=axis):
                face_copy(step, axis, False).start()

    def arrived(step, axes):
        for axis in axes:
            @pl.when(position[axis] > 0)
            def _(axis=axis):
                face_copy(step, axis, True).wait_recv()

            @pl.when(position[axis] < sizes[axis] - 1)
            def _(axis=axis):
                face_copy(step, axis, False).wait_recv()

        low, high = 2 * axes[0], 2 * axes[-1] + 2
        got = recv[step, low:high].reshape((high - low) * face, cols)
        out = dot(scatter[:, low * face : high * face], halves(got))
        return out[:, :cols] + out[:, cols:]

    groups = [(2 * face, 6 * face), (0, 2 * face), (6 * face, 8 * face)]
    starts = [0, 8 * face, 12 * face]

    def load_matrix(which):
        @pl.loop(0, width, unroll=16)
        def _(j):
            rows[pl.ds(pl.multiple_of(j * tiles, tiles), tiles), :] = raw[which][order_ref[j]]

        for (low, high), begin in zip(groups, starts):
            count = high - low
            for c in range(tiles):
                hi, lo = split(rows[pl.ds(low * tiles + c, count, stride=tiles), :])
                mats[which, begin : begin + count, c * lanes : (c + 1) * lanes] = hi
                mats[which, begin + count : begin + 2 * count, c * lanes : (c + 1) * lanes] = lo

    def product(which, vec, factor, step):
        right = halves(vec)
        for g, ((low, high), begin) in enumerate(zip(groups, starts)):
            count = high - low
            out = dot(mats[which, begin : begin + 2 * count], right)
            out = (out[:count, :cols] + (out[:count, cols:] + out[count:, :cols])) * factor
            fresh[low:high] = out
            if g < 2:
                for k in range(low // face, high // face):
                    send[step, k] = out[k * face - low : (k + 1) * face - low]
                start(step, (1, 2) if g == 0 else (0,))

    def natural():
        out = dot(scatter[...], halves(fresh[...]))
        return out[:, :cols] + out[:, cols:]

    def local_dot(left, right):
        return jnp.sum(left * right, axis=0, keepdims=True)

    def sum_copy(turn, level, offset):
        slot = bases[level] + offset
        return pltpu.make_async_remote_copy(
            src_ref=dsend.at[turn, level],
            dst_ref=drecv.at[turn, slot],
            send_sem=dssem.at[turn, slot],
            recv_sem=drsem.at[turn, slot],
            device_id=peer(stages[level], offset),
            device_id_type=MESH,
        )

    def sum_start(turn, level):
        @pl.loop(1, counts[level])
        def _(offset):
            sum_copy(turn, level, offset).start()

    def sum_begin(turn, first, second):
        dsend[turn, 0] = jnp.concatenate([first, second, jnp.zeros((6, cols), F32)], axis=0)
        sum_start(turn, 0)

    def sum_end(turn):
        for level, count in enumerate(counts):
            @pl.loop(1, count)
            def _(offset, level=level):
                sum_copy(turn, level, offset).wait_recv()

            total = dsend[turn, level] + jnp.sum(
                drecv[turn, bases[level] + 1 : bases[level] + count], axis=0
            )
            if level + 1 < len(counts):
                dsend[turn, level + 1] = total
                sum_start(turn, level + 1)
        return total[0:1], total[1:2]

    scale = jnp.full((1, cols), scale_ref[0, 0], F32)
    inverse = 1.0 / scale
    rhs, pre_part, pre, img_part, img, pre2_part, pre2, img2_part = [vecs.at[i] for i in range(8)]

    yz = (1, 2)
    x = (0,)
    load_side.wait()
    post_side()
    pl.semaphore_wait(barrier, sum(counts) - len(counts))
    start(0, yz)
    start(0, x)
    build_scatter()
    for copy in load_inv:
        copy.wait()
    load_matrix(0)
    rhs[...] = side[...] + arrived(0, x)
    rhs[...] += arrived(0, yz)
    product(0, rhs[...], inverse, 1)
    pre_part[...] = natural()
    first = local_dot(rhs[...], pre_part[...])
    for copy in load_schur:
        copy.wait()
    load_matrix(1)
    pre[...] = pre_part[...] + arrived(1, x)
    pre[...] += arrived(1, yz)
    product(1, pre[...], scale, 2)
    img_part[...] = natural()
    second = local_dot(pre[...], img_part[...])
    sum_begin(0, first, second)
    img[...] = img_part[...] + arrived(2, x)
    img[...] += arrived(2, yz)
    product(0, img[...], inverse, 3)
    pre2_part[...] = natural()
    pre2[...] = pre2_part[...] + arrived(3, x)
    pre2[...] += arrived(3, yz)
    product(1, pre2[...], scale, 4)
    img2_part[...] = natural()
    norm_now, along = sum_end(0)
    alpha = norm_now / along
    res_ref[...] = rhs[...] - alpha * img[...]
    sol_ref[...] = pre[...] - alpha * pre2[...]
    sum_begin(
        1,
        local_dot(res_ref[...], pre_part[...] - alpha * pre2_part[...]),
        local_dot(sol_ref[...], img_part[...] - alpha * img2_part[...]),
    )
    img2_part[...] += arrived(4, x)
    image2 = img[...] - alpha * (img2_part[...] + arrived(4, yz))
    norm_next, along = sum_end(1)
    ratio = norm_next / norm_now
    alpha2 = norm_next / (along - ratio * norm_next / alpha)
    sol_ref[...] = alpha * pre[...] + alpha2 * (sol_ref[...] + ratio * pre[...])
    res_ref[...] = res_ref[...] - alpha2 * (image2 + ratio * img[...])

    for step in range(5):
        for axis in range(3):
            @pl.when(position[axis] < sizes[axis] - 1)
            def _(axis=axis):
                face_copy(step, axis, True).wait_send()

            @pl.when(position[axis] > 0)
            def _(axis=axis):
                face_copy(step, axis, False).wait_send()
    for turn in range(2):
        for level, count in enumerate(counts):
            @pl.loop(1, count)
            def _(offset, level=level):
                sum_copy(turn, level, offset).wait_send()


def on_device(local_schur, block_inverse, coefficient, face_index, right_side):
    width = local_schur.shape[0]
    face = width // 8
    cols = right_side.shape[-1]
    sizes = [lax.axis_size(name) for name in AXES]
    total = sizes[0] * sizes[1] * sizes[2]
    stages = [(0, 1, 2)] if total <= 64 else [(0,), (1,), (2,)]
    slots = total if total <= 64 else sum(sizes)
    out = jax.ShapeDtypeStruct((width, cols), F32)
    sol, res = pl.pallas_call(
        functools.partial(kernel, sizes, stages),
        out_shape=(out, out),
        in_specs=[
            pl.BlockSpec(memory_space=pltpu.SMEM),
            pl.BlockSpec(memory_space=pltpu.SMEM),
            pl.BlockSpec(memory_space=pltpu.VMEM),
            pl.BlockSpec(memory_space=pl.ANY),
            pl.BlockSpec(memory_space=pl.ANY),
            pl.BlockSpec(memory_space=pl.ANY),
        ],
        out_specs=(pl.BlockSpec(memory_space=pltpu.VMEM), pl.BlockSpec(memory_space=pltpu.VMEM)),
        scratch_shapes=[
            pltpu.VMEM((width, width // 128, 128), F32),
            pltpu.VMEM((width, width // 128, 128), F32),
            pltpu.VMEM((width * width // 128, 128), F32),
            pltpu.VMEM((width, cols), F32),
            pltpu.VMEM((2, 2 * width, width), BF16),
            pltpu.VMEM((6 * face, width), BF16),
            pltpu.VMEM((width, width), BF16),
            pltpu.VMEM((width, cols), F32),
            pltpu.VMEM((5, 6, face, cols), F32),
            pltpu.VMEM((5, 6, face, cols), F32),
            pltpu.VMEM((8, width, cols), F32),
            pltpu.VMEM((2, len(stages), 8, cols), F32),
            pltpu.VMEM((2, slots, 8, cols), F32),
            pltpu.SemaphoreType.DMA((1 + 2 * (width // 128),)),
            pltpu.SemaphoreType.DMA((5, 6)),
            pltpu.SemaphoreType.DMA((5, 6)),
            pltpu.SemaphoreType.DMA((2, slots)),
            pltpu.SemaphoreType.DMA((2, slots)),
        ],
        compiler_params=pltpu.CompilerParams(
            collective_id=0, has_side_effects=True, vmem_limit_bytes=60 * 1024 * 1024
        ),
        name="schur_pcg",
    )(
        coefficient.reshape(1, 1),
        face_index,
        face_index.reshape(8, face),
        right_side.reshape(width, cols),
        block_inverse,
        local_schur,
    )
    return sol.reshape(1, 1, 1, width, cols), res.reshape(1, 1, 1, width, cols)


def solution(mesh):
    placed = (P(), P(), P(*AXES), P(), P(*AXES, None, None))
    return jax.shard_map(
        on_device,
        mesh=mesh,
        in_specs=placed,
        out_specs=(P(*AXES, None, None), P(*AXES, None, None)),
        check_vma=False,
    )
```

```python
import functools
import jax
import jax.numpy as jnp
from jax import lax
from jax.experimental import pallas as pl
from jax.experimental.pallas import tpu as pltpu
from jax.sharding import PartitionSpec as P

AXES = ("gx", "gy", "gz")
MESH = pl.DeviceIdType.MESH
F32 = jnp.float32
BF16 = jnp.bfloat16


def split(x):
    hi = x.astype(BF16)
    return hi, (x - hi.astype(F32)).astype(BF16)


def halves(x):
    hi, lo = split(x)
    return jnp.concatenate([hi, lo], axis=1)


def dot(a, b):
    return jnp.dot(a, b, preferred_element_type=F32)


def kernel(
    sizes, stages, scale_ref, order_ref, index_ref, side_hbm, inv_hbm, schur_hbm, sol_ref, res_ref,
    raw_inv, raw_schur, rows, side, mats, gather, scatter, fresh, send, recv, vecs, dsend, drecv,
    copy_sem, ssem, rsem, dssem, drsem,
):
    width, cols = side.shape
    face = width // 8
    position = [lax.axis_index(name) for name in AXES]

    load_side = pltpu.make_async_copy(side_hbm, side, copy_sem.at[0])
    raw = (raw_inv, raw_schur)
    lanes = 128
    tiles = width // lanes

    def matrix_copies(which, source):
        return [
            pltpu.make_async_copy(
                source.at[:, c * lanes : (c + 1) * lanes],
                raw[which].at[:, c, :],
                copy_sem.at[1 + which * tiles + c],
            )
            for c in range(tiles)
        ]

    load_inv = matrix_copies(0, inv_hbm)
    load_schur = matrix_copies(1, schur_hbm)
    load_side.start()
    for copy in load_inv + load_schur:
        copy.start()

    def peer(stage, offset):
        count = 1
        me = 0
        for axis in stage:
            count *= sizes[axis]
            me = me * sizes[axis] + position[axis]
        other = lax.rem(me + offset, count)
        device = {}
        for axis in reversed(stage):
            device[AXES[axis]] = lax.rem(other, sizes[axis])
            other = lax.div(other, sizes[axis])
        return device

    counts = []
    for stage in stages:
        count = 1
        for axis in stage:
            count *= sizes[axis]
        counts.append(count)
    bases = [sum(counts[:i]) for i in range(len(counts))]

    barrier = pltpu.get_barrier_semaphore()
    for stage, count in zip(stages, counts):
        @pl.loop(1, count)
        def _(offset, stage=stage):
            pl.semaphore_signal(
                barrier, inc=1, device_id=peer(stage, offset), device_id_type=MESH
            )

    for k in range(6):
        row = index_ref[k : k + 1, :]
        column = jnp.broadcast_to(row.astype(F32), (face, face)).T
        for m in range(width // face):
            across = (lax.broadcasted_iota(jnp.int32, (face, face), 1) + m * face).astype(F32)
            gather[k * face : (k + 1) * face, m * face : (m + 1) * face] = jnp.where(
                across == column, 1.0, 0.0
            ).astype(BF16)

    for axis in range(3):
        @pl.when(position[axis] == 0)
        def _(axis=axis):
            for step in range(5):
                recv[step, 2 * axis] = jnp.zeros((face, cols), F32)

        @pl.when(position[axis] == sizes[axis] - 1)
        def _(axis=axis):
            for step in range(5):
                recv[step, 2 * axis + 1] = jnp.zeros((face, cols), F32)

    def face_copy(step, axis, up):
        mine, theirs = (2 * axis + 1, 2 * axis) if up else (2 * axis, 2 * axis + 1)
        return pltpu.make_async_remote_copy(
            src_ref=send.at[step, mine],
            dst_ref=recv.at[step, theirs],
            send_sem=ssem.at[step, mine],
            recv_sem=rsem.at[step, theirs],
            device_id={AXES[axis]: position[axis] + (1 if up else -1)},
            device_id_type=MESH,
        )

    def post_side():
        out = dot(gather[...], halves(side[...]))
        out = out[:, :cols] + out[:, cols:]
        for k in range(6):
            send[0, k] = out[k * face : (k + 1) * face]

    def build_scatter():
        for k in range(8):
            row = index_ref[k : k + 1, :]
            down = lax.broadcasted_iota(jnp.int32, (width, face), 0)
            scatter[:, k * face : (k + 1) * face] = jnp.where(down == row, 1.0, 0.0).astype(BF16)

    def start(step, axes):
        for axis in axes:
            @pl.when(position[axis] < sizes[axis] - 1)
            def _(axis=axis):
                face_copy(step, axis, True).start()

            @pl.when(position[axis] > 0)
            def _(axis=axis):
                face_copy(step, axis, False).start()

    def arrived(step, axes):
        for axis in axes:
            @pl.when(position[axis] > 0)
            def _(axis=axis):
                face_copy(step, axis, True).wait_recv()

            @pl.when(position[axis] < sizes[axis] - 1)
            def _(axis=axis):
                face_copy(step, axis, False).wait_recv()

        low, high = 2 * axes[0], 2 * axes[-1] + 2
        got = recv[step, low:high].reshape((high - low) * face, cols)
        out = dot(scatter[:, low * face : high * face], halves(got))
        return out[:, :cols] + out[:, cols:]

    groups = [(2 * face, 6 * face), (0, 2 * face), (6 * face, 8 * face)]
    starts = [0, 8 * face, 12 * face]

    def load_matrix(which):
        @pl.loop(0, width, unroll=16)
        def _(j):
            rows[pl.ds(pl.multiple_of(j * tiles, tiles), tiles), :] = raw[which][order_ref[j]]

        for (low, high), begin in zip(groups, starts):
            count = high - low
            for c in range(tiles):
                hi, lo = split(rows[pl.ds(low * tiles + c, count, stride=tiles), :])
                mats[which, begin : begin + count, c * lanes : (c + 1) * lanes] = hi
                mats[which, begin + count : begin + 2 * count, c * lanes : (c + 1) * lanes] = lo

    def product(which, vec, factor, step):
        right = halves(vec)
        for g, ((low, high), begin) in enumerate(zip(groups, starts)):
            count = high - low
            out = dot(mats[which, begin : begin + 2 * count], right)
            out = (out[:count, :cols] + (out[:count, cols:] + out[count:, :cols])) * factor
            fresh[low:high] = out
            if g < 2:
                for k in range(low // face, high // face):
                    send[step, k] = out[k * face - low : (k + 1) * face - low]
                start(step, (1, 2) if g == 0 else (0,))

    def natural():
        out = dot(scatter[...], halves(fresh[...]))
        return out[:, :cols] + out[:, cols:]

    def local_dot(left, right):
        return jnp.sum(left * right, axis=0, keepdims=True)

    def sum_copy(turn, level, offset):
        slot = bases[level] + offset
        return pltpu.make_async_remote_copy(
            src_ref=dsend.at[turn, level],
            dst_ref=drecv.at[turn, slot],
            send_sem=dssem.at[turn, slot],
            recv_sem=drsem.at[turn, slot],
            device_id=peer(stages[level], offset),
            device_id_type=MESH,
        )

    def sum_start(turn, level):
        @pl.loop(1, counts[level])
        def _(offset):
            sum_copy(turn, level, offset).start()

    def sum_begin(turn, first, second):
        dsend[turn, 0] = jnp.concatenate([first, second, jnp.zeros((6, cols), F32)], axis=0)
        sum_start(turn, 0)

    def sum_end(turn):
        for level, count in enumerate(counts):
            @pl.loop(1, count)
            def _(offset, level=level):
                sum_copy(turn, level, offset).wait_recv()

            total = dsend[turn, level] + jnp.sum(
                drecv[turn, bases[level] + 1 : bases[level] + count], axis=0
            )
            if level + 1 < len(counts):
                dsend[turn, level + 1] = total
                sum_start(turn, level + 1)
        return total[0:1], total[1:2]

    scale = jnp.full((1, cols), scale_ref[0, 0], F32)
    inverse = 1.0 / scale
    rhs, pre_part, pre, img_part, img, pre2_part, pre2, img2_part = [vecs.at[i] for i in range(8)]

    yz = (1, 2)
    x = (0,)
    load_side.wait()
    post_side()
    build_scatter()
    pl.semaphore_wait(barrier, sum(counts) - len(counts))
    start(0, yz)
    start(0, x)
    for copy in load_inv:
        copy.wait()
    load_matrix(0)
    rhs[...] = side[...] + arrived(0, x)
    rhs[...] += arrived(0, yz)
    product(0, rhs[...], inverse, 1)
    pre_part[...] = natural()
    first = local_dot(rhs[...], pre_part[...])
    for copy in load_schur:
        copy.wait()
    load_matrix(1)
    pre[...] = pre_part[...] + arrived(1, x)
    pre[...] += arrived(1, yz)
    product(1, pre[...], scale, 2)
    img_part[...] = natural()
    second = local_dot(pre[...], img_part[...])
    sum_begin(0, first, second)
    img[...] = img_part[...] + arrived(2, x)
    img[...] += arrived(2, yz)
    product(0, img[...], inverse, 3)
    pre2_part[...] = natural()
    pre2[...] = pre2_part[...] + arrived(3, x)
    pre2[...] += arrived(3, yz)
    product(1, pre2[...], scale, 4)
    img2_part[...] = natural()
    norm_now, along = sum_end(0)
    alpha = norm_now / along
    res_ref[...] = rhs[...] - alpha * img[...]
    sol_ref[...] = pre[...] - alpha * pre2[...]
    sum_begin(
        1,
        local_dot(res_ref[...], pre_part[...] - alpha * pre2_part[...]),
        local_dot(sol_ref[...], img_part[...] - alpha * img2_part[...]),
    )
    img2_part[...] += arrived(4, x)
    image2 = img[...] - alpha * (img2_part[...] + arrived(4, yz))
    norm_next, along = sum_end(1)
    ratio = norm_next / norm_now
    alpha2 = norm_next / (along - ratio * norm_next / alpha)
    sol_ref[...] = alpha * pre[...] + alpha2 * (sol_ref[...] + ratio * pre[...])
    res_ref[...] = res_ref[...] - alpha2 * (image2 + ratio * img[...])

    for step in range(5):
        for axis in range(3):
            @pl.when(position[axis] < sizes[axis] - 1)
            def _(axis=axis):
                face_copy(step, axis, True).wait_send()

            @pl.when(position[axis] > 0)
            def _(axis=axis):
                face_copy(step, axis, False).wait_send()
    for turn in range(2):
        for level, count in enumerate(counts):
            @pl.loop(1, count)
            def _(offset, level=level):
                sum_copy(turn, level, offset).wait_send()


def hand_on(sol_ref, res_ref, sol_out, res_out):
    sol_out[...] = sol_ref[...]
    res_out[...] = res_ref[...]


def on_device(local_schur, block_inverse, coefficient, face_index, right_side):
    width = local_schur.shape[0]
    face = width // 8
    cols = right_side.shape[-1]
    sizes = [lax.axis_size(name) for name in AXES]
    total = sizes[0] * sizes[1] * sizes[2]
    stages = [(0, 1, 2)] if total <= 64 else [(0,), (1,), (2,)]
    slots = total if total <= 64 else sum(sizes)
    out = jax.ShapeDtypeStruct((width, cols), F32)
    sol, res = pl.pallas_call(
        functools.partial(kernel, sizes, stages),
        out_shape=(out, out),
        in_specs=[
            pl.BlockSpec(memory_space=pltpu.SMEM),
            pl.BlockSpec(memory_space=pltpu.SMEM),
            pl.BlockSpec(memory_space=pltpu.VMEM),
            pl.BlockSpec(memory_space=pl.ANY),
            pl.BlockSpec(memory_space=pl.ANY),
            pl.BlockSpec(memory_space=pl.ANY),
        ],
        out_specs=(pl.BlockSpec(memory_space=pltpu.VMEM), pl.BlockSpec(memory_space=pltpu.VMEM)),
        scratch_shapes=[
            pltpu.VMEM((width, width // 128, 128), F32),
            pltpu.VMEM((width, width // 128, 128), F32),
            pltpu.VMEM((width * width // 128, 128), F32),
            pltpu.VMEM((width, cols), F32),
            pltpu.VMEM((2, 2 * width, width), BF16),
            pltpu.VMEM((6 * face, width), BF16),
            pltpu.VMEM((width, width), BF16),
            pltpu.VMEM((width, cols), F32),
            pltpu.VMEM((5, 6, face, cols), F32),
            pltpu.VMEM((5, 6, face, cols), F32),
            pltpu.VMEM((8, width, cols), F32),
            pltpu.VMEM((2, len(stages), 8, cols), F32),
            pltpu.VMEM((2, slots, 8, cols), F32),
            pltpu.SemaphoreType.DMA((1 + 2 * (width // 128),)),
            pltpu.SemaphoreType.DMA((5, 6)),
            pltpu.SemaphoreType.DMA((5, 6)),
            pltpu.SemaphoreType.DMA((2, slots)),
            pltpu.SemaphoreType.DMA((2, slots)),
        ],
        compiler_params=pltpu.CompilerParams(
            collective_id=0, has_side_effects=True, vmem_limit_bytes=60 * 1024 * 1024
        ),
        name="schur_pcg",
    )(
        coefficient.reshape(1, 1),
        face_index,
        face_index.reshape(8, face),
        right_side.reshape(width, cols),
        block_inverse,
        local_schur,
    )
    block = pl.BlockSpec((width // 2, cols), lambda i: (i, 0))
    sol, res = pl.pallas_call(
        hand_on,
        grid=(2,),
        out_shape=(out, out),
        in_specs=[block, block],
        out_specs=(block, block),
        name="hand_on",
    )(sol, res)
    return sol.reshape(1, 1, 1, width, cols), res.reshape(1, 1, 1, width, cols)


def solution(mesh):
    placed = (P(), P(), P(*AXES), P(), P(*AXES, None, None))
    return jax.shard_map(
        on_device,
        mesh=mesh,
        in_specs=placed,
        out_specs=(P(*AXES, None, None), P(*AXES, None, None)),
        check_vma=False,
    )
```
